32 devices in a mesh: groups: 2 (over y), replay: 4 (over z), module: 2 (over x), half: 2 (over core).
Axes of the slice: x: 2, y: 2, z: 4, core: 2. Of those that a mesh axis runs over, the one named last changes fastest.
Arguments:
- new_factors: bfloat16 [128, 2, 64, 128], P(('groups', 'replay', 'module')), parts along dimension 0, may hold values from -0.5 to 0.5
- new_counts: int32 [128], P(('groups', 'replay', 'module')), parts along dimension 0, may hold values from 32 to 64
- new_ids: int32 [128], P(('groups', 'module', 'half')), parts along dimension 0, may hold values from 0 to 3071
- replay_grads: bfloat16 [6144, 2, 4096], P(('groups', 'replay'), 'module', 'half'), parts along dimension 0, may hold values from -0.75 to 0.75
- replay_ids: int32 [6144], P(('groups', 'replay')), parts along dimension 0, may hold values from 0 to 3071
- slot_module: int32 [2], replicated, may hold values from 0 to 1, each once
- output_inverse: float32 [2, 64, 64], replicated, as said below
- input_inverse: float32 [2, 64, 64], replicated, as said below
Outputs:
- scores: float32 [128, 3072], P(('groups', 'module', 'half'), 'replay'), parts along dimension 0
The draws below stay inside these ranges and needn't reach their ends.
There are 2 independent parts, one for each index of `groups`. The reference program is written for one: setup_inputs(seed, part) draws one part's arguments, and reference() takes and returns one part's arrays. A program takes and returns all parts, laid end to end along the dimension named above; an argument that names none is the same for every part. Nothing has to cross between parts.
Inputs may be any that keep to these rules, and one draw needn't show every extreme that they name: `new_counts`: each new example has at least half of its token slots live, the live ones first. `slot_module`: each module sits in exactly one slot. `output_inverse`: symmetric with a positive diagonal. `input_inverse`: symmetric with a positive diagonal.
All inputs are finite; a program needn't handle non-finite values.
Results may differ from the reference program's by a relative error of at most 0.0029.
Values may be sent and summed in bfloat16 or wider, within the bound.
A program may use at most 64 MiB of HBM per device.

```python
import jax
import jax.numpy as jnp
from jax import lax

FEAT = 64
TOK = 64
MODULES = 2
NEW_TOTAL = 64
REPLAY_TOTAL = 3072


def inverse_factor(key, salt):
    seed_key = jax.random.fold_in(key, salt)
    diagonal_key, spread_key = jax.random.split(seed_key)
    eye_mask = jnp.eye(FEAT, dtype=jnp.float32)
    diagonal = jnp.exp(jax.random.uniform(diagonal_key, (MODULES, FEAT), jnp.float32, -0.7, 0.7))
    spread_part = 0.1 * jax.random.normal(spread_key, (MODULES, FEAT, FEAT), jnp.float32)
    symmetric = 0.7071 * (spread_part + jnp.swapaxes(spread_part, 1, 2))
    return symmetric * (1.0 - eye_mask) + diagonal[:, :, None] * eye_mask


def draw_output_inverse(key, part):
    return inverse_factor(key, 11)


def draw_input_inverse(key, part):
    return inverse_factor(key, 23)


def place_ends(result, key, low, top_value):
    extent = result.shape
    place = [jax.random.randint(jax.random.fold_in(key, axis), (), 0, extent[axis]) for axis in range(len(extent))]
    result = result.at[tuple(place)].set(low)
    longest = extent.index(max(extent))
    place[longest] = (place[longest] + 1) % extent[longest]
    return result.at[tuple(place)].set(top_value)


def block_scale(own_key, dims, pieces, least, high):
    def one(dim, blocks):
        steps = jax.random.uniform(jax.random.fold_in(jax.random.fold_in(own_key, 6), dim), (blocks,), jnp.float32, least / len(pieces), high / len(pieces))
        return jnp.repeat(jnp.exp(steps), dims[dim] // blocks).reshape((-1,) + (1,) * (len(dims) - dim - 1))

    loudness = one(*pieces[0])
    for cut in pieces[1:]:
        loudness = loudness * one(*cut)
    return loudness


def normal_values(stream_key, shape, spread, limit, shards=(), held_as=jnp.bfloat16):
    entries = jax.random.normal(stream_key, shape, jnp.float32) * spread
    if len(shards) > 0:
        entries = block_scale(stream_key, shape, shards, -0.22, 0.18) * entries
    return jnp.clip(entries, min=-limit, max=limit).astype(held_as)


def setup_inputs(seed: int = 0, part: int = 0) -> dict:
    splits = jax.random.split(jax.random.key(seed), 9)
    part_splits = jax.random.split(jax.random.fold_in(splits[8], part), 9)
    return {
        "new_factors": normal_values(part_splits[0], (NEW_TOTAL, MODULES, TOK, 2 * FEAT), 0.08, 0.5, ((0, 8),)),
        "new_counts": place_ends(jax.random.randint(part_splits[1], (NEW_TOTAL,), TOK // 2, TOK + 1), jax.random.fold_in(part_splits[1], 1), TOK // 2, TOK).astype(jnp.int32),
        "new_ids": place_ends(jax.random.randint(part_splits[2], (NEW_TOTAL,), 0, REPLAY_TOTAL), jax.random.fold_in(part_splits[2], 1), 0, REPLAY_TOTAL - 1).astype(jnp.int32),
        "replay_grads": normal_values(part_splits[3], (REPLAY_TOTAL, MODULES, FEAT * FEAT), 0.125, 0.75, ((0, 4), (1, 2), (2, 2))),
        "replay_ids": place_ends(jax.random.randint(part_splits[4], (REPLAY_TOTAL,), 0, REPLAY_TOTAL), jax.random.fold_in(part_splits[4], 1), 0, REPLAY_TOTAL - 1).astype(jnp.int32),
        "slot_module": jax.random.permutation(splits[5], MODULES).astype(jnp.int32),
        "output_inverse": draw_output_inverse(jax.random.fold_in(splits[8], 71), part),
        "input_inverse": draw_input_inverse(jax.random.fold_in(splits[8], 71), part),
    }


def reference(new_factors, new_counts, new_ids, replay_grads, replay_ids, slot_module, output_inverse, input_inverse):
    token_index = jnp.arange(TOK, dtype=jnp.int32)
    token_live = token_index[None, :] < new_counts[:, None]
    live_factors = jnp.where(token_live[:, None, :, None], new_factors, jnp.zeros((), jnp.bfloat16))
    raw = jnp.zeros((NEW_TOTAL, REPLAY_TOTAL), jnp.float32)
    for slot_index in range(MODULES):
        module_index = slot_module[slot_index]
        chosen = jnp.take(live_factors, module_index, axis=1)
        activations = chosen[:, :, :FEAT].astype(jnp.float32)
        output_grads = chosen[:, :, FEAT:].astype(jnp.float32)
        gradients = jnp.einsum('ntr,ntc->nrc', output_grads, activations)
        left_inverse = jnp.take(output_inverse, module_index, axis=0)
        right_inverse = jnp.take(input_inverse, module_index, axis=0)
        preconditioned = jnp.einsum('rk,nkc->nrc', left_inverse, gradients, precision=lax.Precision.HIGHEST)
        preconditioned = jnp.einsum('nrk,kc->nrc', preconditioned, right_inverse, precision=lax.Precision.HIGHEST)
        preconditioned = preconditioned.astype(jnp.bfloat16).reshape(NEW_TOTAL, FEAT * FEAT)
        raw = raw + lax.dot_general(preconditioned, replay_grads[:, slot_index, :], (((1,), (1,)), ((), ())), preferred_element_type=jnp.float32)
    self_pairs = new_ids[:, None] == replay_ids[None, :]
    return jnp.where(self_pairs, jnp.zeros((), jnp.float32), raw)
```

```python
import functools

import jax
import jax.numpy as jnp
from jax import lax
from jax.experimental import pallas as pl
from jax.experimental.pallas import tpu as pltpu
from jax.sharding import PartitionSpec as P

MESH = pl.DeviceIdType.MESH
UNROLL = 16
PIECES = 2
TERM = jnp.bfloat16


def each(count, step):
    if count <= UNROLL:
        for index in range(count):
            step(index)
    else:
        def one(index, carry):
            step(index)
            return carry

        lax.fori_loop(0, count, one, 0)


def parts_of(value):
    high = value.astype(jnp.bfloat16)
    low = (value - high.astype(jnp.float32)).astype(jnp.bfloat16)
    return high, low


def kernel(
    sizes,
    slot_module_hbm,
    counts_hbm,
    factors_hbm,
    replay_hbm,
    left_hbm,
    right_hbm,
    out_ref,
    slot_module,
    counts,
    factors,
    replay,
    replay_t,
    inverses,
    rows_f32,
    outgoing,
    blocks,
    part,
    terms,
    arrived,
    load_sem,
    ready,
    send_sem,
    recv_sem,
    score_recv_sem,
):
    replays, modules, halves, chunk = sizes
    z, x, h = lax.axis_index("replay"), lax.axis_index("module"), lax.axis_index("half")
    block = z * modules + x
    owner = x * halves + h
    owners = modules * halves
    examples, _, tokens, width = factors.shape
    feat = width // 2
    share = replay.shape[1] // feat
    columns = replay.shape[0]
    chunks = columns // chunk
    last = replays - 1

    left, right = inverses.at[0], inverses.at[1]
    for source, target, index in (
        (factors_hbm, factors, 0),
        (left_hbm, left, 1),
        (right_hbm, right, 1),
        (slot_module_hbm, slot_module, 2),
        (counts_hbm, counts, 3),
    ):
        pltpu.make_async_copy(source, target, load_sem.at[index]).start()
    replay_load = pltpu.make_async_copy(replay_hbm, replay, load_sem.at[4])
    replay_load.start()

    barrier = pltpu.get_barrier_semaphore()

    def tell(semaphore, device):
        pl.semaphore_signal(semaphore, inc=1, device_id=device, device_id_type=MESH)

    def place(index):
        return index // halves * halves + halves - 1 - lax.rem(index, halves)

    for offset in range(1, owners):
        index = lax.rem(owner + offset, owners)

        @pl.when(place(owner) < place(index))
        def _():
            tell(barrier, {"module": index // halves, "half": lax.rem(index, halves)})

    def greet_above(index):
        @pl.when(index + 1 > z)
        def _():
            for slot in range(modules):
                tell(barrier, {"replay": index + 1, "module": slot})

    each(last, greet_above)
    def landed(ref, semaphore):
        pltpu.make_async_copy(ref, ref, semaphore).wait()

    landed(factors, load_sem.at[0])
    landed(inverses, load_sem.at[1])
    landed(slot_module, load_sem.at[2])
    landed(counts, load_sem.at[3])

    pair = 128 // tokens
    lane = lax.broadcasted_iota(jnp.int32, (share, 128), 1)
    low_lanes = lax.broadcasted_iota(jnp.int32, (examples, 2 * feat), 1) < feat

    def factored(slot):
        module = slot_module[slot]
        entries = factors[:, module].reshape(examples * tokens, width)
        doubled = jnp.concatenate([entries, entries], axis=1)
        right_high, right_low = parts_of(right[module])
        blank = jnp.zeros((feat, feat), jnp.bfloat16)
        right_rows = jnp.concatenate([right_high, blank, right_low, blank], axis=0)
        right_rows = jnp.concatenate([right_rows, right_rows], axis=1)
        v = jnp.dot(doubled, right_rows, preferred_element_type=jnp.float32)
        left_high, left_low = parts_of(left[module, pl.ds(pl.multiple_of(h * share, share), share), :])
        left_blank = jnp.zeros((share, feat), jnp.bfloat16)
        left_columns = jnp.concatenate([left_blank, left_high, left_blank, left_low], axis=1)
        u = lax.dot_general(
            left_columns, doubled, (((1,), (1,)), ((), ())), preferred_element_type=jnp.float32
        )
        return u, v

    def precondition(slot, u, v):
        v_high, v_low = parts_of(v)
        for group in range(examples // pair):
            u_pair = u[:, group * 128 : (group + 1) * 128]
            masked = []
            for inner in range(pair):
                count = counts[group * pair + inner]
                first = inner * tokens
                keep = (lane >= first) & (lane < first + count)
                masked.append(jnp.where(keep, u_pair, 0.0))
            u_high, u_low = parts_of(jnp.concatenate(masked, axis=0))
            lhs = jnp.concatenate([u_high, u_high, u_low], axis=1)
            span = slice(group * 128, (group + 1) * 128)
            rhs = jnp.concatenate([v_high[span], v_low[span], v_high[span]], axis=0)
            rows_f32[pl.ds(group * pair * share, pair * share), :] = jnp.dot(
                lhs, rhs, preferred_element_type=jnp.float32
            )
        for q in range(share // 2):
            even = rows_f32[pl.ds(2 * q, examples, stride=share), :]
            odd = rows_f32[pl.ds(2 * q + 1, examples, stride=share), :]
            outgoing[slot, :, q * 2 * feat : (q + 1) * 2 * feat] = jnp.where(low_lanes, even, odd).astype(
                jnp.bfloat16
            )

    def block_copy(slot, target_z):
        return pltpu.make_async_remote_copy(
            src_ref=outgoing.at[slot],
            dst_ref=blocks.at[block],
            send_sem=send_sem.at[0],
            recv_sem=recv_sem.at[z],
            device_id={"replay": target_z, "module": slot},
            device_id_type=MESH,
        )

    through = h == halves - 1
    skips_first = through & (z > 1)
    skips_last = through & (z < last - 1)
    hands_down = through & (z == 1) & (last > 1)
    hands_up = through & (z == last - 1) & (last > 1)

    def relay_copy(source, target_z, semaphore):
        return pltpu.make_async_remote_copy(
            src_ref=blocks.at[source],
            dst_ref=blocks.at[source],
            send_sem=semaphore,
            recv_sem=recv_sem.at[source // modules],
            device_id={"replay": target_z},
            device_id_type=MESH,
        )

    def hand_on(source_z):
        for step, semaphore, hands in ((-1, send_sem.at[2], hands_down & (source_z > z)), (1, send_sem.at[3], hands_up & (source_z < z))):

            @pl.when(hands)
            def _():
                for slot in range(modules):
                    relay_copy(source_z * modules + slot, z + step, semaphore).start()

    others = [lax.rem(x + offset, modules) for offset in range(1, modules)]

    def send_below(slot):
        def to(index):
            @pl.when((index < z) & jnp.logical_not(skips_first & (index == 0)))
            def _():
                block_copy(slot, index).start()

        each(last, to)

    def send_above(index):
        @pl.when(index + 1 > z)
        def _():
            pl.semaphore_wait(ready.at[index + 1], modules)

        @pl.when((index + 1 > z) & jnp.logical_not(skips_last & (index + 1 == last)))
        def _():
            for slot in [x, *others]:
                block_copy(slot, index + 1).start()

    order = [x, *others]
    factorings = [factored(slot) for slot in order]

    earlier = place(owner) + modules * z

    @pl.when(earlier > 0)
    def _():
        pl.semaphore_wait(barrier, earlier)

    for offset in range(1, owners):
        index = lax.rem(owner + offset, owners)

        @pl.when(place(owner) > place(index))
        def _():
            tell(ready.at[z], {"module": index // halves, "half": lax.rem(index, halves)})

    def answer_below(index):
        @pl.when(index < z)
        def _():
            for slot in range(modules):
                tell(ready.at[z], {"replay": index, "module": slot})

    each(last, answer_below)

    for index, slot in enumerate(order):
        precondition(slot, *factorings[index])
        send_below(slot)
        if index == 0:
            blocks[block] = outgoing[x]

    later = owners - 1 - place(owner)

    @pl.when(later > 0)
    def _():
        pl.semaphore_wait(ready.at[z], later)

    for slot in others:
        block_copy(slot, z).start()

    per_owner = replays // owners
    step_rows = modules * examples

    def await_plane(source_z):
        landed(blocks.at[pl.ds(source_z * modules, modules)], recv_sem.at[source_z])

    def score_copy(source, c):
        cut = pl.ds(c * chunk, chunk)
        target = source // per_owner
        return pltpu.make_async_remote_copy(
            src_ref=terms.at[pl.ds(pl.multiple_of(source * step_rows, step_rows), step_rows), cut],
            dst_ref=arrived.at[
                owner, pl.ds(pl.multiple_of((source % per_owner) * step_rows, step_rows), step_rows), cut
            ],
            send_sem=send_sem.at[1],
            recv_sem=score_recv_sem.at[c],
            device_id={"module": target // halves, "half": target % halves},
            device_id_type=MESH,
        )

    replay_load.wait()
    for first in range(0, replay.shape[1], 256):
        span = slice(first, first + 256)
        replay_t[span, :] = replay[:, span].T

    def score(planes):
        lhs = jnp.concatenate(
            [blocks[source * modules + slot] for source in planes for slot in range(modules)], axis=0
        )
        for c in range(chunks):
            cut = slice(c * chunk, (c + 1) * chunk)
            scores = jnp.dot(lhs, replay_t[:, cut], preferred_element_type=jnp.float32)
            for inner, source in enumerate(planes):
                rows = pl.ds(pl.multiple_of(source * step_rows, step_rows), step_rows)
                own = scores[inner * step_rows : (inner + 1) * step_rows]
                part[rows, cut] = own
                terms[rows, cut] = own.astype(terms.dtype)

                @pl.when(source // per_owner != owner)
                def _():
                    score_copy(source, c).start()

    each(last, send_above)
    landed(blocks.at[pl.ds(0, modules - 1)], recv_sem.at[z])
    score([z])

    def source_of(index):
        both = jnp.minimum(z, last - z)
        paired = index < 2 * both
        distance = jnp.where(paired, index // 2 + 1, index - both + 1)
        below = jnp.where(paired, 1 - index % 2, jnp.where(2 * z > last, 1, 0))
        return z + distance * (1 - 2 * below)

    def arrivals(first, count):
        planes = [source_of(first + inner) for inner in range(count)]
        for source_z in planes:
            await_plane(source_z)
            hand_on(source_z)
        score(planes)

    single = last % 2
    if single:
        arrivals(0, 1)
    each(last // 2, lambda index: arrivals(single + 2 * index, 2))

    for c in range(chunks):
        cut = slice(c * chunk, (c + 1) * chunk)
        landed(arrived.at[pl.ds(0, owners - 1), :, cut], score_recv_sem.at[c])
        first = owner * per_owner * step_rows
        summed = part[pl.ds(pl.multiple_of(first, step_rows), per_owner * step_rows), cut]
        for offset in range(1, owners):
            summed = summed + arrived[lax.rem(owner + offset, owners), :, cut].astype(jnp.float32)
        out_ref[:, cut] = summed

    skipped = jnp.where(skips_first, 1, 0) + jnp.where(skips_last, 1, 0)
    for planes in range(min(3, replays)):

        @pl.when(skipped == planes)
        def _():
            landed(blocks.at[pl.ds(0, (replays - planes) * modules - 1)], send_sem.at[0])

    for hands, semaphore in ((hands_down, send_sem.at[2]), (hands_up, send_sem.at[3])):
        if last > 1:

            @pl.when(hands)
            def _():
                landed(blocks.at[pl.ds(0, (last - 1) * modules)], semaphore)

    landed(terms.at[pl.ds(0, (replays - per_owner) * step_rows)], send_sem.at[1])


def pin(array):
    return pltpu.with_memory_space_constraint(array, pltpu.HBM)


def body(
    replays,
    modules,
    halves,
    new_factors,
    new_counts,
    new_ids,
    replay_grads,
    replay_ids,
    slot_module,
    output_inverse,
    input_inverse,
):
    examples, _, _, width = new_factors.shape
    feat = width // 2
    columns, _, depth = replay_grads.shape
    share = depth // feat
    total = replays * modules * examples
    owners = modules * halves
    rows = total // owners
    chunk = 384 if columns % 384 == 0 else columns // PIECES
    hbm = pl.BlockSpec(memory_space=pltpu.HBM)
    summed = pl.pallas_call(
        functools.partial(kernel, (replays, modules, halves, chunk)),
        out_shape=jax.ShapeDtypeStruct((rows, columns), jnp.float32),
        in_specs=[hbm] * 6,
        out_specs=pl.BlockSpec(memory_space=pltpu.VMEM),
        scratch_shapes=[
            pltpu.SMEM(slot_module.shape, jnp.int32),
            pltpu.SMEM(new_counts.shape, jnp.int32),
            pltpu.VMEM(new_factors.shape, jnp.bfloat16),
            pltpu.VMEM((columns, depth), jnp.bfloat16),
            pltpu.VMEM((depth, columns), jnp.bfloat16),
            pltpu.VMEM((2, *output_inverse.shape), jnp.float32),
            pltpu.VMEM((examples * share, 2 * feat), jnp.float32),
            pltpu.VMEM((modules, examples, depth), jnp.bfloat16),
            pltpu.VMEM((replays * modules, examples, depth), jnp.bfloat16),
            pltpu.VMEM((total, columns), jnp.float32),
            pltpu.VMEM((total, columns), TERM),
            pltpu.VMEM((owners, rows, columns), TERM),
            pltpu.SemaphoreType.DMA((5,)),
            pltpu.SemaphoreType.REGULAR((replays,)),
            pltpu.SemaphoreType.DMA((4,)),
            pltpu.SemaphoreType.DMA((replays,)),
            pltpu.SemaphoreType.DMA((columns // chunk,)),
        ],
        compiler_params=pltpu.CompilerParams(
            collective_id=0, has_side_effects=True, vmem_limit_bytes=32 * 1024 * 1024
        ),
        name="attribution",
    )(
        pin(slot_module),
        pin(new_counts),
        pin(new_factors),
        pin(replay_grads.reshape(columns, depth)),
        pin(output_inverse),
        pin(input_inverse),
    )
    self_pairs = new_ids[:, None] == replay_ids[None, :]
    return jnp.where(self_pairs, jnp.zeros((), jnp.float32), summed)


def solution(mesh):
    in_specs = (
        P(("groups", "replay", "module"), None, None, None),
        P(("groups", "replay", "module")),
        P(("groups", "module", "half")),
        P(("groups", "replay"), "module", "half"),
        P(("groups", "replay")),
        P(),
        P(),
        P(),
    )
    out_specs = P(("groups", "module", "half"), "replay")
    return jax.shard_map(
        functools.partial(body, mesh.shape["replay"], mesh.shape["module"], mesh.shape["half"]),
        mesh=mesh,
        in_specs=in_specs,
        out_specs=out_specs,
        check_vma=False,
    )
```

```python
import functools

import jax
import jax.numpy as jnp
from jax import lax
from jax.experimental import pallas as pl
from jax.experimental.pallas import tpu as pltpu
from jax.sharding import PartitionSpec as P

MESH = pl.DeviceIdType.MESH
UNROLL = 16
PIECES = 2
TERM = jnp.bfloat16


def each(count, step):
    if count <= UNROLL:
        for index in range(count):
            step(index)
    else:
        def one(index, carry):
            step(index)
            return carry

        lax.fori_loop(0, count, one, 0)


def parts_of(value):
    high = value.astype(jnp.bfloat16)
    low = (value - high.astype(jnp.float32)).astype(jnp.bfloat16)
    return high, low


def kernel(
    sizes,
    slot_module_hbm,
    counts_hbm,
    factors_hbm,
    replay_hbm,
    left_hbm,
    right_hbm,
    out_ref,
    slot_module,
    counts,
    factors,
    replay,
    replay_t,
    inverses,
    rows_f32,
    outgoing,
    blocks,
    part,
    terms,
    arrived,
    load_sem,
    ready,
    send_sem,
    recv_sem,
    score_recv_sem,
):
    replays, modules, halves, chunk = sizes
    z, x, h = lax.axis_index("replay"), lax.axis_index("module"), lax.axis_index("half")
    block = z * modules + x
    owner = x * halves + h
    owners = modules * halves
    examples, _, tokens, width = factors.shape
    feat = width // 2
    share = replay.shape[1] // feat
    columns = replay.shape[0]
    chunks = columns // chunk
    last = replays - 1

    left, right = inverses.at[0], inverses.at[1]
    for source, target, index in (
        (factors_hbm, factors, 0),
        (left_hbm, left, 1),
        (right_hbm, right, 1),
        (slot_module_hbm, slot_module, 2),
        (counts_hbm, counts, 3),
    ):
        pltpu.make_async_copy(source, target, load_sem.at[index]).start()
    replay_load = pltpu.make_async_copy(replay_hbm, replay, load_sem.at[4])
    replay_load.start()

    barrier = pltpu.get_barrier_semaphore()

    def tell(semaphore, device):
        pl.semaphore_signal(semaphore, inc=1, device_id=device, device_id_type=MESH)

    def place(index):
        return index // halves * halves + halves - 1 - lax.rem(index, halves)

    for offset in range(1, owners):
        index = lax.rem(owner + offset, owners)

        @pl.when(place(owner) < place(index))
        def _():
            tell(barrier, {"module": index // halves, "half": lax.rem(index, halves)})

    def greet_above(index):
        @pl.when(index + 1 > z)
        def _():
            for slot in range(modules):
                tell(barrier, {"replay": index + 1, "module": slot})

    each(last, greet_above)
    def enter():
        earlier = place(owner) + modules * z

        @pl.when(earlier > 0)
        def _():
            pl.semaphore_wait(barrier, earlier)

        for offset in range(1, owners):
            index = lax.rem(owner + offset, owners)

            @pl.when(place(owner) > place(index))
            def _():
                tell(ready.at[z], {"module": index // halves, "half": lax.rem(index, halves)})

        def answer_below(index):
            @pl.when(index < z)
            def _():
                for slot in range(modules):
                    tell(ready.at[z], {"replay": index, "module": slot})

        each(last, answer_below)

    @pl.when(x > 0)
    def _():
        enter()

    def landed(ref, semaphore):
        pltpu.make_async_copy(ref, ref, semaphore).wait()

    landed(factors, load_sem.at[0])
    landed(inverses, load_sem.at[1])
    landed(slot_module, load_sem.at[2])
    landed(counts, load_sem.at[3])

    pair = 128 // tokens
    lane = lax.broadcasted_iota(jnp.int32, (share, 128), 1)
    low_lanes = lax.broadcasted_iota(jnp.int32, (examples, 2 * feat), 1) < feat

    def factored(slot):
        module = slot_module[slot]
        entries = factors[:, module].reshape(examples * tokens, width)
        doubled = jnp.concatenate([entries, entries], axis=1)
        right_high, right_low = parts_of(right[module])
        blank = jnp.zeros((feat, feat), jnp.bfloat16)
        right_rows = jnp.concatenate([right_high, blank, right_low, blank], axis=0)
        right_rows = jnp.concatenate([right_rows, right_rows], axis=1)
        v = jnp.dot(doubled, right_rows, preferred_element_type=jnp.float32)
        left_high, left_low = parts_of(left[module, pl.ds(pl.multiple_of(h * share, share), share), :])
        left_blank = jnp.zeros((share, feat), jnp.bfloat16)
        left_columns = jnp.concatenate([left_blank, left_high, left_blank, left_low], axis=1)
        u = lax.dot_general(
            left_columns, doubled, (((1,), (1,)), ((), ())), preferred_element_type=jnp.float32
        )
        return u, v

    def precondition(slot, u, v):
        v_high, v_low = parts_of(v)
        for group in range(examples // pair):
            u_pair = u[:, group * 128 : (group + 1) * 128]
            masked = []
            for inner in range(pair):
                count = counts[group * pair + inner]
                first = inner * tokens
                keep = (lane >= first) & (lane < first + count)
                masked.append(jnp.where(keep, u_pair, 0.0))
            u_high, u_low = parts_of(jnp.concatenate(masked, axis=0))
            lhs = jnp.concatenate([u_high, u_high, u_low], axis=1)
            span = slice(group * 128, (group + 1) * 128)
            rhs = jnp.concatenate([v_high[span], v_low[span], v_high[span]], axis=0)
            rows_f32[pl.ds(group * pair * share, pair * share), :] = jnp.dot(
                lhs, rhs, preferred_element_type=jnp.float32
            )
        for q in range(share // 2):
            even = rows_f32[pl.ds(2 * q, examples, stride=share), :]
            odd = rows_f32[pl.ds(2 * q + 1, examples, stride=share), :]
            outgoing[slot, :, q * 2 * feat : (q + 1) * 2 * feat] = jnp.where(low_lanes, even, odd).astype(
                jnp.bfloat16
            )

    def block_copy(slot, target_z):
        return pltpu.make_async_remote_copy(
            src_ref=outgoing.at[slot],
            dst_ref=blocks.at[block],
            send_sem=send_sem.at[0],
            recv_sem=recv_sem.at[z],
            device_id={"replay": target_z, "module": slot},
            device_id_type=MESH,
        )

    through = h == halves - 1
    skips_first = through & (z > 1)
    skips_last = through & (z < last - 1)
    hands_down = through & (z == 1) & (last > 1)
    hands_up = through & (z == last - 1) & (last > 1)

    def relay_copy(source, target_z, semaphore):
        return pltpu.make_async_remote_copy(
            src_ref=blocks.at[source],
            dst_ref=blocks.at[source],
            send_sem=semaphore,
            recv_sem=recv_sem.at[source // modules],
            device_id={"replay": target_z},
            device_id_type=MESH,
        )

    def handed_on(source_z):
        return (hands_down & (source_z > z)) | (hands_up & (source_z < z))

    def hand_on(source_z):
        for step, semaphore, hands in ((-1, send_sem.at[2], hands_down & (source_z > z)), (1, send_sem.at[3], hands_up & (source_z < z))):

            @pl.when(hands)
            def _():
                for slot in range(modules):
                    relay_copy(source_z * modules + slot, z + step, semaphore).start()

    others = [lax.rem(x + offset, modules) for offset in range(1, modules)]

    def send_below(slot):
        def to(index):
            @pl.when((index < z) & jnp.logical_not(skips_first & (index == 0)))
            def _():
                block_copy(slot, index).start()

        each(last, to)

    def send_above(index):
        @pl.when(index + 1 > z)
        def _():
            pl.semaphore_wait(ready.at[index + 1], modules)

        @pl.when((index + 1 > z) & jnp.logical_not(skips_last & (index + 1 == last)))
        def _():
            for slot in order:
                block_copy(slot, index + 1).start()

    order = [*others, x]
    factorings = [factored(slot) for slot in order]

    @pl.when(x == 0)
    def _():
        enter()

    for index, slot in enumerate(order):
        precondition(slot, *factorings[index])
        send_below(slot)

    per_owner = replays // owners
    step_rows = modules * examples

    def await_plane(source_z):
        landed(blocks.at[pl.ds(source_z * modules, modules)], recv_sem.at[source_z])

    def score_copy(source, c):
        cut = pl.ds(c * chunk, chunk)
        target = source // per_owner
        return pltpu.make_async_remote_copy(
            src_ref=terms.at[pl.ds(pl.multiple_of(source * step_rows, step_rows), step_rows), cut],
            dst_ref=arrived.at[
                owner, pl.ds(pl.multiple_of((source % per_owner) * step_rows, step_rows), step_rows), cut
            ],
            send_sem=send_sem.at[1],
            recv_sem=score_recv_sem.at[c],
            device_id={"module": target // halves, "half": target % halves},
            device_id_type=MESH,
        )

    replay_load.wait()
    for first in range(0, replay.shape[1], 256):
        span = slice(first, first + 256)
        replay_t[span, :] = replay[:, span].T

    blocks[block] = outgoing[x]
    later = owners - 1 - place(owner)

    @pl.when(later > 0)
    def _():
        pl.semaphore_wait(ready.at[z], later)

    for slot in others:
        block_copy(slot, z).start()

    def score(planes):
        lhs = jnp.concatenate(
            [blocks[source * modules + slot] for source in planes for slot in range(modules)], axis=0
        )
        for c in range(chunks):
            cut = slice(c * chunk, (c + 1) * chunk)
            scores = jnp.dot(lhs, replay_t[:, cut], preferred_element_type=jnp.float32)
            for inner, source in enumerate(planes):
                rows = pl.ds(pl.multiple_of(source * step_rows, step_rows), step_rows)
                own = scores[inner * step_rows : (inner + 1) * step_rows]
                part[rows, cut] = own
                terms[rows, cut] = own.astype(terms.dtype)

                @pl.when(source // per_owner != owner)
                def _():
                    score_copy(source, c).start()

    def source_of(index):
        both = jnp.minimum(z, last - z)
        paired = index < 2 * both
        distance = jnp.where(paired, index // 2 + 1, index - both + 1)
        below = jnp.where(paired, 1 - index % 2, jnp.where(2 * z > last, 1, 0))
        return z + distance * (1 - 2 * below)

    each(last, send_above)

    def hand_over(index):
        source_z = source_of(index)

        @pl.when(handed_on(source_z))
        def _():
            await_plane(source_z)
            hand_on(source_z)

    each(last, hand_over)
    landed(blocks.at[pl.ds(0, modules - 1)], recv_sem.at[z])
    score([z])

    def arrivals(first, count):
        planes = [source_of(first + inner) for inner in range(count)]
        for source_z in planes:

            @pl.when(jnp.logical_not(handed_on(source_z)))
            def _():
                await_plane(source_z)

        score(planes)

    single = last % 2
    if single:
        arrivals(0, 1)
    each(last // 2, lambda index: arrivals(single + 2 * index, 2))

    for c in range(chunks):
        cut = slice(c * chunk, (c + 1) * chunk)
        landed(arrived.at[pl.ds(0, owners - 1), :, cut], score_recv_sem.at[c])
        first = owner * per_owner * step_rows
        summed = part[pl.ds(pl.multiple_of(first, step_rows), per_owner * step_rows), cut]
        for offset in range(1, owners):
            summed = summed + arrived[lax.rem(owner + offset, owners), :, cut].astype(jnp.float32)
        out_ref[:, cut] = summed

    skipped = jnp.where(skips_first, 1, 0) + jnp.where(skips_last, 1, 0)
    for planes in range(min(3, replays)):

        @pl.when(skipped == planes)
        def _():
            landed(blocks.at[pl.ds(0, (replays - planes) * modules - 1)], send_sem.at[0])

    for hands, semaphore in ((hands_down, send_sem.at[2]), (hands_up, send_sem.at[3])):
        if last > 1:

            @pl.when(hands)
            def _():
                landed(blocks.at[pl.ds(0, (last - 1) * modules)], semaphore)

    landed(terms.at[pl.ds(0, (replays - per_owner) * step_rows)], send_sem.at[1])


def pin(array):
    return pltpu.with_memory_space_constraint(array, pltpu.HBM)


def body(
    replays,
    modules,
    halves,
    new_factors,
    new_counts,
    new_ids,
    replay_grads,
    replay_ids,
    slot_module,
    output_inverse,
    input_inverse,
):
    examples, _, _, width = new_factors.shape
    feat = width // 2
    columns, _, depth = replay_grads.shape
    share = depth // feat
    total = replays * modules * examples
    owners = modules * halves
    rows = total // owners
    chunk = 384 if columns % 384 == 0 else columns // PIECES
    hbm = pl.BlockSpec(memory_space=pltpu.HBM)
    summed = pl.pallas_call(
        functools.partial(kernel, (replays, modules, halves, chunk)),
        out_shape=jax.ShapeDtypeStruct((rows, columns), jnp.float32),
        in_specs=[hbm] * 6,
        out_specs=pl.BlockSpec(memory_space=pltpu.VMEM),
        scratch_shapes=[
            pltpu.SMEM(slot_module.shape, jnp.int32),
            pltpu.SMEM(new_counts.shape, jnp.int32),
            pltpu.VMEM(new_factors.shape, jnp.bfloat16),
            pltpu.VMEM((columns, depth), jnp.bfloat16),
            pltpu.VMEM((depth, columns), jnp.bfloat16),
            pltpu.VMEM((2, *output_inverse.shape), jnp.float32),
            pltpu.VMEM((examples * share, 2 * feat), jnp.float32),
            pltpu.VMEM((modules, examples, depth), jnp.bfloat16),
            pltpu.VMEM((replays * modules, examples, depth), jnp.bfloat16),
            pltpu.VMEM((total, columns), jnp.float32),
            pltpu.VMEM((total, columns), TERM),
            pltpu.VMEM((owners, rows, columns), TERM),
            pltpu.SemaphoreType.DMA((5,)),
            pltpu.SemaphoreType.REGULAR((replays,)),
            pltpu.SemaphoreType.DMA((4,)),
            pltpu.SemaphoreType.DMA((replays,)),
            pltpu.SemaphoreType.DMA((columns // chunk,)),
        ],
        compiler_params=pltpu.CompilerParams(
            collective_id=0, has_side_effects=True, vmem_limit_bytes=32 * 1024 * 1024
        ),
        name="attribution",
    )(
        pin(slot_module),
        pin(new_counts),
        pin(new_factors),
        pin(replay_grads.reshape(columns, depth)),
        pin(output_inverse),
        pin(input_inverse),
    )
    self_pairs = new_ids[:, None] == replay_ids[None, :]
    return jnp.where(self_pairs, jnp.zeros((), jnp.float32), summed)


def solution(mesh):
    in_specs = (
        P(("groups", "replay", "module"), None, None, None),
        P(("groups", "replay", "module")),
        P(("groups", "module", "half")),
        P(("groups", "replay"), "module", "half"),
        P(("groups", "replay")),
        P(),
        P(),
        P(),
    )
    out_specs = P(("groups", "module", "half"), "replay")
    return jax.shard_map(
        functools.partial(body, mesh.shape["replay"], mesh.shape["module"], mesh.shape["half"]),
        mesh=mesh,
        in_specs=in_specs,
        out_specs=out_specs,
        check_vma=False,
    )
```

```python
import functools

import jax
import jax.numpy as jnp
from jax import lax
from jax.experimental import pallas as pl
from jax.experimental.pallas import tpu as pltpu
from jax.sharding import PartitionSpec as P

MESH = pl.DeviceIdType.MESH
UNROLL = 16
PIECES = 2
TERM = jnp.bfloat16


def each(count, step):
    if count <= UNROLL:
        for index in range(count):
            step(index)
    else:
        def one(index, carry):
            step(index)
            return carry

        lax.fori_loop(0, count, one, 0)


def parts_of(value):
    high = value.astype(jnp.bfloat16)
    low = (value - high.astype(jnp.float32)).astype(jnp.bfloat16)
    return high, low


def kernel(
    sizes,
    slot_module_hbm,
    counts_hbm,
    factors_hbm,
    replay_hbm,
    left_hbm,
    right_hbm,
    out_ref,
    slot_module,
    counts,
    factors,
    replay,
    replay_t,
    inverses,
    rows_f32,
    outgoing,
    blocks,
    part,
    terms,
    arrived,
    load_sem,
    ready,
    send_sem,
    recv_sem,
    score_recv_sem,
):
    replays, modules, halves, chunk = sizes
    z, x, h = lax.axis_index("replay"), lax.axis_index("module"), lax.axis_index("half")
    block = z * modules + x
    owner = x * halves + h
    owners = modules * halves
    examples, _, tokens, width = factors.shape
    feat = width // 2
    share = replay.shape[1] // feat
    columns = replay.shape[0]
    chunks = columns // chunk
    last = replays - 1

    left, right = inverses.at[0], inverses.at[1]
    for source, target, index in (
        (factors_hbm, factors, 0),
        (left_hbm, left, 1),
        (right_hbm, right, 1),
        (slot_module_hbm, slot_module, 2),
        (counts_hbm, counts, 3),
    ):
        pltpu.make_async_copy(source, target, load_sem.at[index]).start()
    replay_load = pltpu.make_async_copy(replay_hbm, replay, load_sem.at[4])
    replay_load.start()

    barrier = pltpu.get_barrier_semaphore()

    def tell(semaphore, device):
        pl.semaphore_signal(semaphore, inc=1, device_id=device, device_id_type=MESH)

    others = [lax.rem(x + offset, modules) for offset in range(1, modules)]

    def place(index):
        return index // halves * halves + halves - 1 - lax.rem(index, halves)

    for offset in range(1, owners):
        index = lax.rem(owner + offset, owners)

        @pl.when(place(owner) < place(index))
        def _():
            tell(barrier, {"module": index // halves, "half": lax.rem(index, halves)})

    def greet_above(index):
        @pl.when(index + 1 > z)
        def _():
            for slot in range(modules):
                tell(barrier, {"replay": index + 1, "module": slot})

    each(last, greet_above)

    @pl.when(z > 0)
    def _():
        tell(barrier, {"replay": z - 1})

    def enter():
        earlier = place(owner) + modules * z + jnp.where(z < last, 1, 0)

        @pl.when(earlier > 0)
        def _():
            pl.semaphore_wait(barrier, earlier)

        for offset in range(1, owners):
            index = lax.rem(owner + offset, owners)

            @pl.when(place(owner) > place(index))
            def _():
                tell(ready.at[z], {"module": index // halves, "half": lax.rem(index, halves)})

        def answer_below(index):
            @pl.when(index < z)
            def _():
                for slot in others:
                    tell(ready.at[z], {"replay": index, "module": slot})

            @pl.when(index < z - 1)
            def _():
                tell(ready.at[z], {"replay": index})

        each(last, answer_below)

    @pl.when(x > 0)
    def _():
        enter()

    def landed(ref, semaphore):
        pltpu.make_async_copy(ref, ref, semaphore).wait()

    landed(factors, load_sem.at[0])
    landed(inverses, load_sem.at[1])
    landed(slot_module, load_sem.at[2])
    landed(counts, load_sem.at[3])

    pair = 128 // tokens
    lane = lax.broadcasted_iota(jnp.int32, (share, 128), 1)
    low_lanes = lax.broadcasted_iota(jnp.int32, (examples, 2 * feat), 1) < feat

    def precondition(slot):
        module = slot_module[slot]
        entries = factors[:, module].reshape(examples * tokens, width)
        doubled = jnp.concatenate([entries, entries], axis=1)
        right_high, right_low = parts_of(right[module])
        blank = jnp.zeros((feat, feat), jnp.bfloat16)
        right_rows = jnp.concatenate([right_high, blank, right_low, blank], axis=0)
        right_rows = jnp.concatenate([right_rows, right_rows], axis=1)
        v = jnp.dot(doubled, right_rows, preferred_element_type=jnp.float32)
        left_high, left_low = parts_of(left[module, pl.ds(pl.multiple_of(h * share, share), share), :])
        left_blank = jnp.zeros((share, feat), jnp.bfloat16)
        left_columns = jnp.concatenate([left_blank, left_high, left_blank, left_low], axis=1)
        u = lax.dot_general(
            left_columns, doubled, (((1,), (1,)), ((), ())), preferred_element_type=jnp.float32
        )
        v_high, v_low = parts_of(v)
        for group in range(examples // pair):
            u_pair = u[:, group * 128 : (group + 1) * 128]
            masked = []
            for inner in range(pair):
                count = counts[group * pair + inner]
                first = inner * tokens
                keep = (lane >= first) & (lane < first + count)
                masked.append(jnp.where(keep, u_pair, 0.0))
            u_high, u_low = parts_of(jnp.concatenate(masked, axis=0))
            lhs = jnp.concatenate([u_high, u_high, u_low], axis=1)
            span = slice(group * 128, (group + 1) * 128)
            rhs = jnp.concatenate([v_high[span], v_low[span], v_high[span]], axis=0)
            rows_f32[pl.ds(group * pair * share, pair * share), :] = jnp.dot(
                lhs, rhs, preferred_element_type=jnp.float32
            )
        for q in range(share // 2):
            even = rows_f32[pl.ds(2 * q, examples, stride=share), :]
            odd = rows_f32[pl.ds(2 * q + 1, examples, stride=share), :]
            outgoing[slot, :, q * 2 * feat : (q + 1) * 2 * feat] = jnp.where(low_lanes, even, odd).astype(
                jnp.bfloat16
            )

    def block_copy(slot, target_z):
        return pltpu.make_async_remote_copy(
            src_ref=outgoing.at[slot],
            dst_ref=blocks.at[block],
            send_sem=send_sem.at[0],
            recv_sem=recv_sem.at[z],
            device_id={"replay": target_z, "module": slot},
            device_id_type=MESH,
        )

    through = h == halves - 1
    skips_first = through & (z > 1)
    skips_last = through & (z < last - 1)
    hands_down = through & (z == 1) & (last > 1)
    hands_up = through & (z == last - 1) & (last > 1)

    def relay_copy(source, target_z, semaphore):
        return pltpu.make_async_remote_copy(
            src_ref=blocks.at[source],
            dst_ref=blocks.at[source],
            send_sem=semaphore,
            recv_sem=recv_sem.at[source // modules],
            device_id={"replay": target_z},
            device_id_type=MESH,
        )

    def handed_on(source_z):
        return (hands_down & (source_z > z)) | (hands_up & (source_z < z))

    def hand_on(source_z):
        for step, semaphore, hands in ((-1, send_sem.at[2], hands_down & (source_z > z)), (1, send_sem.at[3], hands_up & (source_z < z))):

            @pl.when(hands)
            def _():
                for slot in range(modules):
                    relay_copy(source_z * modules + slot, z + step, semaphore).start()


    def send_below(slot):
        def to(index):
            @pl.when((index < z) & jnp.logical_not(skips_first & (index == 0)))
            def _():
                block_copy(slot, index).start()

        each(last, to)

    def send_above(index):
        answers = modules - 1 + jnp.where(index > z, 1, 0)

        @pl.when((index + 1 > z) & (answers > 0))
        def _():
            pl.semaphore_wait(ready.at[index + 1], answers)

        @pl.when((index + 1 > z) & jnp.logical_not(skips_last & (index + 1 == last)))
        def _():
            for slot in others:
                block_copy(slot, index + 1).start()

        @pl.when((index > z) & jnp.logical_not(skips_last & (index + 1 == last)))
        def _():
            block_copy(x, index + 1).start()

    order = [*others, x]
    for index, slot in enumerate(order):
        precondition(slot)
        if index == 0:

            @pl.when(x == 0)
            def _():
                enter()

        send_below(slot)
        if index == modules - 1:

            @pl.when(z < last)
            def _():
                block_copy(x, z + 1).start()

        else:

            @pl.when(slot < x)
            def _():
                block_copy(slot, z).start()


    per_owner = replays // owners
    step_rows = modules * examples

    def await_plane(source_z):
        landed(blocks.at[pl.ds(source_z * modules, modules)], recv_sem.at[source_z])

    def score_copy(source, c):
        cut = pl.ds(c * chunk, chunk)
        target = source // per_owner
        return pltpu.make_async_remote_copy(
            src_ref=terms.at[pl.ds(pl.multiple_of(source * step_rows, step_rows), step_rows), cut],
            dst_ref=arrived.at[
                owner, pl.ds(pl.multiple_of((source % per_owner) * step_rows, step_rows), step_rows), cut
            ],
            send_sem=send_sem.at[1],
            recv_sem=score_recv_sem.at[c],
            device_id={"module": target // halves, "half": target % halves},
            device_id_type=MESH,
        )

    replay_load.wait()
    for first in range(0, replay.shape[1], 256):
        span = slice(first, first + 256)
        replay_t[span, :] = replay[:, span].T

    blocks[block] = outgoing[x]
    later = owners - 1 - place(owner)

    @pl.when(later > 0)
    def _():
        pl.semaphore_wait(ready.at[z], later)

    for slot in others:

        @pl.when(slot > x)
        def _():
            block_copy(slot, z).start()


    middle = replay_t.shape[0] // 2

    def product(lhs, start):
        span = slice(start, start + 128)
        first = jnp.dot(lhs[:, :middle], replay_t[:middle, span], preferred_element_type=jnp.float32)
        return first + jnp.dot(lhs[:, middle:], replay_t[middle:, span], preferred_element_type=jnp.float32)

    def score(planes):
        lhs = jnp.concatenate(
            [blocks[source * modules + slot] for source in planes for slot in range(modules)], axis=0
        )
        for c in range(chunks):
            cut = slice(c * chunk, (c + 1) * chunk)
            scores = jnp.concatenate([product(lhs, start) for start in range(c * chunk, (c + 1) * chunk, 128)], axis=1)
            for inner, source in enumerate(planes):
                rows = pl.ds(pl.multiple_of(source * step_rows, step_rows), step_rows)
                own = scores[inner * step_rows : (inner + 1) * step_rows]
                part[rows, cut] = own
                terms[rows, cut] = own.astype(terms.dtype)

                @pl.when(source // per_owner != owner)
                def _():
                    score_copy(source, c).start()

    def source_of(index):
        both = jnp.minimum(z, last - z)
        paired = index < 2 * both
        distance = jnp.where(paired, index // 2 + 1, index - both + 1)
        below = jnp.where(paired, 1 - index % 2, jnp.where(2 * z > last, 1, 0))
        return z + distance * (1 - 2 * below)

    each(last, send_above)

    def hand_over(index):
        source_z = source_of(index)

        @pl.when(handed_on(source_z))
        def _():
            await_plane(source_z)
            hand_on(source_z)

    each(last, hand_over)

    def await_other(source_z):
        @pl.when(jnp.logical_not(handed_on(source_z)))
        def _():
            await_plane(source_z)

    if last:
        await_other(source_of(0))
    landed(blocks.at[pl.ds(0, modules - 1)], recv_sem.at[z])
    score([z, source_of(0)] if last else [z])

    def arrivals(first, count):
        planes = [source_of(first + inner) for inner in range(count)]

        @pl.when(through)
        def _():
            for source_z in planes:
                await_other(source_z)
                score([source_z])

        @pl.when(jnp.logical_not(through))
        def _():
            for source_z in planes:
                await_other(source_z)
            score(planes)

    each((last - 1) // 2, lambda index: arrivals(1 + 2 * index, 2))
    if last > 1 and last % 2 == 0:
        arrivals(last - 1, 1)

    for c in range(chunks):
        cut = slice(c * chunk, (c + 1) * chunk)
        landed(arrived.at[pl.ds(0, owners - 1), :, cut], score_recv_sem.at[c])
        first = owner * per_owner * step_rows
        summed = part[pl.ds(pl.multiple_of(first, step_rows), per_owner * step_rows), cut]
        for offset in range(1, owners):
            summed = summed + arrived[lax.rem(owner + offset, owners), :, cut].astype(jnp.float32)
        out_ref[:, cut] = summed

    skipped = jnp.where(skips_first, 1, 0) + jnp.where(skips_last, 1, 0)
    for planes in range(min(3, replays)):

        @pl.when(skipped == planes)
        def _():
            landed(blocks.at[pl.ds(0, (replays - planes) * modules - 1)], send_sem.at[0])

    for hands, semaphore in ((hands_down, send_sem.at[2]), (hands_up, send_sem.at[3])):
        if last > 1:

            @pl.when(hands)
            def _():
                landed(blocks.at[pl.ds(0, (last - 1) * modules)], semaphore)

    landed(terms.at[pl.ds(0, (replays - per_owner) * step_rows)], send_sem.at[1])


def pin(array):
    return pltpu.with_memory_space_constraint(array, pltpu.HBM)


def body(
    replays,
    modules,
    halves,
    new_factors,
    new_counts,
    new_ids,
    replay_grads,
    replay_ids,
    slot_module,
    output_inverse,
    input_inverse,
):
    examples, _, _, width = new_factors.shape
    feat = width // 2
    columns, _, depth = replay_grads.shape
    share = depth // feat
    total = replays * modules * examples
    owners = modules * halves
    rows = total // owners
    chunk = 384 if columns % 384 == 0 else columns // PIECES
    hbm = pl.BlockSpec(memory_space=pltpu.HBM)
    summed = pl.pallas_call(
        functools.partial(kernel, (replays, modules, halves, chunk)),
        out_shape=jax.ShapeDtypeStruct((rows, columns), jnp.float32),
        in_specs=[hbm] * 6,
        out_specs=pl.BlockSpec(memory_space=pltpu.VMEM),
        scratch_shapes=[
            pltpu.SMEM(slot_module.shape, jnp.int32),
            pltpu.SMEM(new_counts.shape, jnp.int32),
            pltpu.VMEM(new_factors.shape, jnp.bfloat16),
            pltpu.VMEM((columns, depth), jnp.bfloat16),
            pltpu.VMEM((depth, columns), jnp.bfloat16),
            pltpu.VMEM((2, *output_inverse.shape), jnp.float32),
            pltpu.VMEM((examples * share, 2 * feat), jnp.float32),
            pltpu.VMEM((modules, examples, depth), jnp.bfloat16),
            pltpu.VMEM((replays * modules, examples, depth), jnp.bfloat16),
            pltpu.VMEM((total, columns), jnp.float32),
            pltpu.VMEM((total, columns), TERM),
            pltpu.VMEM((owners, rows, columns), TERM),
            pltpu.SemaphoreType.DMA((5,)),
            pltpu.SemaphoreType.REGULAR((replays,)),
            pltpu.SemaphoreType.DMA((4,)),
            pltpu.SemaphoreType.DMA((replays,)),
            pltpu.SemaphoreType.DMA((columns // chunk,)),
        ],
        compiler_params=pltpu.CompilerParams(
            collective_id=0, has_side_effects=True, vmem_limit_bytes=32 * 1024 * 1024
        ),
        name="attribution",
    )(
        pin(slot_module),
        pin(new_counts),
        pin(new_factors),
        pin(replay_grads.reshape(columns, depth)),
        pin(output_inverse),
        pin(input_inverse),
    )
    self_pairs = new_ids[:, None] == replay_ids[None, :]
    return jnp.where(self_pairs, jnp.zeros((), jnp.float32), summed)


def solution(mesh):
    in_specs = (
        P(("groups", "replay", "module"), None, None, None),
        P(("groups", "replay", "module")),
        P(("groups", "module", "half")),
        P(("groups", "replay"), "module", "half"),
        P(("groups", "replay")),
        P(),
        P(),
        P(),
    )
    out_specs = P(("groups", "module", "half"), "replay")
    return jax.shard_map(
        functools.partial(body, mesh.shape["replay"], mesh.shape["module"], mesh.shape["half"]),
        mesh=mesh,
        in_specs=in_specs,
        out_specs=out_specs,
        check_vma=False,
    )
```
